32 devices in a mesh: dp: 8 (over y, x, core), tensor: 4 (over z).
Axes of the slice: x: 2, y: 2, z: 4, core: 2. Of those that a mesh axis runs over, the one named last changes fastest.
Arguments:
- tokens: bfloat16 [2048, 3072], P('dp', 'tensor'), may hold values from -6 to 6
- blocks: bfloat16 [3, 3072, 3072], P(None, 'tensor'), may hold values from -0.125 to 0.125
- left_factor: bfloat16 [3072, 256], P('tensor'), may hold values from -0.109375 to 0.109375
- right_factor: bfloat16 [256, 12288], P(None, 'tensor'), may hold values from -0.375 to 0.375
- upstream: bfloat16 [2048, 12288], P('dp', 'tensor'), may hold values from -6 to 6
Outputs:
- activated: bfloat16 [2048, 12288], P('dp', 'tensor')
- token_grad: bfloat16 [2048, 3072], P('dp', 'tensor')
- left_grad: bfloat16 [3072, 256], P('tensor')
- right_grad: bfloat16 [256, 12288], P(None, 'tensor')
The draws below stay inside these ranges and needn't reach their ends.
All inputs are finite; a program needn't handle non-finite values.
Results may differ from the reference program's by a relative error of at most 0.0063.
Values may be sent and summed in bfloat16 or wider, within the bound.
No kernel may reach another device: no remote copies, remote signals or barrier semaphores. Data moves between devices by JAX's collectives and lax.ppermute only.
A program may use at most 128 MiB of HBM per device.

```python
import jax
import jax.numpy as jnp

DB = 768
FB = 3072
R = 256
SOURCES = 3
D = 3072
FF = 12288
TOKENS = 2048
N_TENSOR = 4


def level_of(rng, extent, pieces, low, top_value):
    level = 1.0
    for axis_at, shards_of in pieces:
        draws = jax.random.uniform(jax.random.fold_in(jax.random.fold_in(rng, 6), axis_at), (shards_of,), jnp.float32, low / len(pieces), top_value / len(pieces))
        level = level * jnp.repeat(jnp.exp(draws), extent[axis_at] // shards_of).reshape((-1,) + (1,) * (len(extent) - 1 - axis_at))
    return level


def gaussian(stream_key, extent, deviation, limit, split=(), held_as=jnp.bfloat16):
    values = deviation * jax.random.normal(stream_key, extent, jnp.float32)
    if split:
        values = values * level_of(stream_key, extent, split, -0.22, 0.18)
    return jnp.clip(values, -limit, limit).astype(held_as)


def setup_inputs(seed: int = 0) -> dict:
    key_list = jax.random.split(jax.random.key(seed), 6)
    return {
        "tokens": gaussian(key_list[0], (TOKENS, D), 1.0, 6.0, ((0, 8), (1, 4))),
        "blocks": gaussian(key_list[1], (SOURCES, D, FB), (SOURCES * DB) ** -0.5, 0.125, ((1, 4),)),
        "left_factor": gaussian(key_list[2], (D, R), D ** -0.5, 0.109375, ((0, 4),)),
        "right_factor": gaussian(key_list[3], (R, FF), R ** -0.5, 0.375, ((1, 4),)),
        "upstream": gaussian(key_list[4], (TOKENS, FF), 1.0, 6.0, ((0, 8), (1, 4))),
    }


def reference(tokens, blocks, left_factor, right_factor, upstream):
    block_count = N_TENSOR
    levels = blocks.shape[0] - 1
    slabs = tokens.reshape(TOKENS, block_count, DB)
    weights = blocks.reshape(levels + 1, block_count, DB, FB)
    low_rank = jnp.dot(tokens, left_factor, preferred_element_type=jnp.float32).astype(jnp.bfloat16)
    expanded = jnp.dot(low_rank, right_factor, preferred_element_type=jnp.float32).reshape(TOKENS, block_count, FB)
    outputs = []
    for column in range(block_count):
        running = expanded[:, column]
        for section in range(levels + 1):
            source = column if section == 0 else column ^ 1 << section - 1
            running = running + jnp.dot(slabs[:, source], weights[section, column], preferred_element_type=jnp.float32)
        outputs.append(running)
    preact = jnp.stack(outputs, 1).reshape(TOKENS, FF)
    gelu_out, pullback = jax.vjp(jax.nn.gelu, preact)
    activated = gelu_out.astype(jnp.bfloat16)
    slopes = pullback(upstream.astype(jnp.float32))[0].astype(jnp.bfloat16)
    mixed_rows = jnp.dot(slopes, right_factor.T, preferred_element_type=jnp.float32).astype(jnp.bfloat16)
    slope_blocks = slopes.reshape(TOKENS, block_count, FB)
    left_blocks = left_factor.reshape(block_count, DB, R)
    grads = []
    for source in range(block_count):
        running = jnp.dot(mixed_rows, left_blocks[source].T, preferred_element_type=jnp.float32)
        for section in range(levels + 1):
            column = source if section == 0 else source ^ 1 << section - 1
            running = running + jnp.dot(slope_blocks[:, column], weights[section, column].T, preferred_element_type=jnp.float32)
        grads.append(running)
    token_grad = jnp.stack(grads, 1).reshape(TOKENS, D).astype(jnp.bfloat16)
    norm_scale = 1.0 / jnp.sqrt(jnp.float32(TOKENS))
    left_grad = (jnp.dot(tokens.T, mixed_rows, preferred_element_type=jnp.float32) * norm_scale).astype(jnp.bfloat16)
    right_grad = (jnp.dot(low_rank.T, slopes, preferred_element_type=jnp.float32) * norm_scale).astype(jnp.bfloat16)
    return (activated, token_grad, left_grad, right_grad)
```

```python
import jax
import jax.numpy as jnp
from jax import lax
from jax.sharding import PartitionSpec as P


def swap(block, axis, mask):
    count = lax.axis_size(axis)
    route = [(i, i ^ mask) for i in range(count)]
    return lax.ppermute(block, axis, route)


def across(left, right, left_dim, right_dim):
    return lax.dot_general(
        left, right, (((left_dim,), (right_dim,)), ((), ())), preferred_element_type=jnp.float32
    )


def sum_over(value, axis):
    mask = 1
    while mask < lax.axis_size(axis):
        value = value + swap(value.astype(jnp.bfloat16), axis, mask).astype(jnp.float32)
        mask *= 2
    return value


def rows_of(value, index, height):
    return lax.dynamic_slice_in_dim(value, index * height, height, 0)


def total_over(value, scale, axis):
    count = lax.axis_size(axis)
    if count & (count - 1) or count < 4 or value.shape[0] % (16 * count):
        return (lax.psum(value, axis) * scale).astype(jnp.bfloat16)
    me = lax.axis_index(axis)
    core = me & 1
    chip = me >> 1
    chips = count // 2
    half = value.shape[0] // 2
    piece = half // chips
    sent = rows_of(value, 1 - core, half).astype(jnp.bfloat16)
    mine = rows_of(value, core, half) + swap(sent, axis, 1).astype(jnp.float32)
    parts = [
        swap(rows_of(mine, chip ^ other, piece).astype(jnp.bfloat16), axis, 2 * other)
        for other in range(1, chips)
    ]
    whole = rows_of(mine, chip, piece)
    for part in parts:
        whole = whole + part.astype(jnp.float32)
    whole = (whole * scale).astype(jnp.bfloat16)
    pieces = [whole] + [swap(whole, axis, 2 * other) for other in range(1, chips)]
    gathered = jnp.zeros((half, value.shape[1]), jnp.bfloat16)
    for other, part in enumerate(pieces):
        gathered = lax.dynamic_update_slice_in_dim(gathered, part, (chip ^ other) * piece, 0)
    result = jnp.zeros(value.shape, jnp.bfloat16)
    result = lax.dynamic_update_slice_in_dim(result, gathered, core * half, 0)
    return lax.dynamic_update_slice_in_dim(
        result, swap(gathered, axis, 1), (1 - core) * half, 0
    )


def body(tokens, blocks, left_factor, right_factor, upstream):
    levels = blocks.shape[0] - 1
    row_count = tokens.shape[0]
    low_part = jnp.dot(tokens, left_factor, preferred_element_type=jnp.float32)
    low_rank = sum_over(low_part, "tensor").astype(jnp.bfloat16)
    preact = jnp.dot(tokens, blocks[0], preferred_element_type=jnp.float32)
    for bit_index in range(levels):
        partner = swap(tokens, "tensor", 1 << bit_index)
        preact = preact + jnp.dot(
            partner, blocks[bit_index + 1], preferred_element_type=jnp.float32
        )
    preact = preact + jnp.dot(low_rank, right_factor, preferred_element_type=jnp.float32)
    gelu_out, pullback = jax.vjp(jax.nn.gelu, preact)
    activated = gelu_out.astype(jnp.bfloat16)
    slopes = pullback(upstream.astype(jnp.float32))[0].astype(jnp.bfloat16)
    norm_scale = 1.0 / jnp.sqrt(jnp.float32(row_count * lax.axis_size("dp")))
    mixed_rows = sum_over(across(slopes, right_factor, 1, 1), "tensor").astype(jnp.bfloat16)
    right_grad = total_over(across(low_rank, slopes, 0, 0), norm_scale, "dp")
    running = across(slopes, blocks[0], 1, 1)
    for bit_index in range(levels):
        partial_value = across(slopes, blocks[bit_index + 1], 1, 1).astype(jnp.bfloat16)
        running = running + swap(partial_value, "tensor", 1 << bit_index).astype(jnp.float32)
    token_grad = (running + across(mixed_rows, left_factor, 1, 1)).astype(jnp.bfloat16)
    left_grad = total_over(across(tokens, mixed_rows, 0, 0), norm_scale, "dp")
    return activated, token_grad, left_grad, right_grad


def solution(mesh):
    placed = (
        P("dp", "tensor"),
        P(None, "tensor", None),
        P("tensor", None),
        P(None, "tensor"),
        P("dp", "tensor"),
    )
    return jax.shard_map(
        body,
        mesh=mesh,
        in_specs=placed,
        out_specs=(P("dp", "tensor"), P("dp", "tensor"), P("tensor", None), P(None, "tensor")),
        check_vma=False,
    )
```

```python
import functools

import jax
import jax.numpy as jnp
from jax import lax
from jax.experimental import pallas as pl
from jax.experimental.pallas import tpu as pltpu
from jax.sharding import PartitionSpec as P


VMEM = pl.BlockSpec(memory_space=pltpu.VMEM)
SMEM = pl.BlockSpec(memory_space=pltpu.SMEM)
HBM = pl.BlockSpec(memory_space=pltpu.HBM)
MIB = 1 << 20


def swap(block, axes, partner):
    dp, tensor = lax.axis_size("dp"), lax.axis_size("tensor")
    if axes == "dp":
        route = [(i, partner(i, 0)) for i in range(dp)]
    else:
        axes = ("dp", "tensor")
        route = [(i * tensor + j, i * tensor + partner(i, j)) for i in range(dp) for j in range(tensor)]
    return lax.ppermute(block, axes, route)


def swap_tensor(block, step, levels):
    return swap(block, "tensor", lambda i, j: j ^ (1 << (levels - 1 - step if i & 1 else step)))


def swap_chips(block, step, count):
    return swap(block, "dp", lambda i, j: i ^ (2 << (count - 1 - step if i & 1 else step)))


def swap_core(block):
    return swap(block, "dp", lambda i, j: i ^ 1)


def dot(left, right, left_dim, right_dim):
    return lax.dot_general(
        left, right, (((left_dim,), (right_dim,)), ((), ())), preferred_element_type=jnp.float32
    )


def tiles(extent, width):
    return [slice(at, min(at + width, extent)) for at in range(0, extent, width)]


def call(kernel, outs, args, flops, mib, scratch=(), in_specs=None, out_specs=None):
    nbytes = sum(a.size * a.dtype.itemsize for a in (*args, *outs))
    return pl.pallas_call(
        kernel,
        out_shape=outs,
        in_specs=in_specs or [VMEM] * len(args),
        out_specs=out_specs or [VMEM] * len(outs),
        scratch_shapes=list(scratch),
        compiler_params=pltpu.CompilerParams(vmem_limit_bytes=mib * MIB),
        cost_estimate=pl.CostEstimate(flops=flops, bytes_accessed=nbytes // 8, transcendentals=0),
    )(*args)


def chip_at(device, side, chips, position):
    steps = chips.bit_length() - 1
    core = (device & 1) ^ side
    up = down = 0
    for step in range(steps):
        if position >> (steps - 1 - step) & 1:
            up |= 1 << step
            down |= 1 << (steps - 1 - step)
    return (device >> 1) ^ (up + core * (down - up))


def section_at(device, step, levels):
    return step + 1 + (device & 1) * (levels - 1 - 2 * step)


def low_kernel(device_ref, x_ref, left_ref, total_ref, sent_ref):
    value = dot(x_ref[...], left_ref[...], 1, 0)
    total_ref[...] = value
    sent_ref[...] = value.astype(jnp.bfloat16)


def low_partial(device, tokens, left_factor):
    shape = (tokens.shape[0], left_factor.shape[1])
    outs = [jax.ShapeDtypeStruct(shape, jnp.float32), jax.ShapeDtypeStruct(shape, jnp.bfloat16)]
    flops = 2 * tokens.size * shape[1]
    specs = [SMEM, VMEM, VMEM]
    return call(low_kernel, outs, (device, tokens, left_factor), flops, 4, (), specs)


def add_kernel(value_ref, got_ref, total_ref, sent_ref):
    value = value_ref[...] + got_ref[...].astype(jnp.float32)
    total_ref[...] = value
    sent_ref[...] = value.astype(jnp.bfloat16)


def add(value, got):
    outs = [
        jax.ShapeDtypeStruct(value.shape, jnp.float32),
        jax.ShapeDtypeStruct(value.shape, jnp.bfloat16),
    ]
    return call(add_kernel, outs, (value, got), 0, 2)


def first_kernel(device_ref, x_ref, b_ref, out_ref, held_ref, sem):
    copies = []
    columns = tiles(out_ref.shape[1], 512)
    for index, at in enumerate(columns):
        copies.append(
            pltpu.make_async_copy(b_ref.at[0, :, at], held_ref.at[0, :, at], sem.at[index])
        )
    for section in range(1, b_ref.shape[0]):
        copies.append(
            pltpu.make_async_copy(
                b_ref.at[section], held_ref.at[section], sem.at[len(columns) + section - 1]
            )
        )
    for copy in copies:
        copy.start()
    x = x_ref[...]
    for copy, at in zip(copies, columns):
        copy.wait()
        out_ref[:, at] = dot(x, held_ref[0, :, at], 1, 0)
    for copy in copies[len(columns) :]:
        copy.wait()


def first(device, tokens, blocks):
    outs = [
        jax.ShapeDtypeStruct((tokens.shape[0], blocks.shape[2]), jnp.float32),
        jax.ShapeDtypeStruct(blocks.shape, blocks.dtype),
    ]
    count = len(tiles(blocks.shape[2], 512)) + blocks.shape[0] - 1
    scratch = [pltpu.SemaphoreType.DMA((count,))]
    flops = 2 * tokens.size * blocks.shape[2]
    return call(first_kernel, outs, (device, tokens, blocks), flops, 34, scratch, [SMEM, VMEM, HBM])


def forward_kernel(step, device_ref, x_ref, b_ref, running_ref, out_ref):
    section = section_at(device_ref[0], step, b_ref.shape[0] - 1)
    x = x_ref[...]
    for at in tiles(out_ref.shape[1], 512):
        out_ref[:, at] = running_ref[:, at] + dot(x, b_ref[section, :, at], 1, 0)


def forward(device, step, x, blocks, running):
    out = jax.ShapeDtypeStruct(running.shape, jnp.float32)
    flops = 2 * x.size * blocks.shape[2]
    kernel = functools.partial(forward_kernel, step)
    specs = [SMEM, VMEM, VMEM, VMEM]
    return call(kernel, [out], (device, x, blocks, running), flops, 4, (), specs)[0]


def backward_kernel(step, device_ref, s_ref, b_ref, out_ref):
    section = 0 if step is None else section_at(device_ref[0], step, b_ref.shape[0] - 1)
    slopes = s_ref[...]
    for at in tiles(out_ref.shape[1], 256):
        out_ref[:, at] = dot(slopes, b_ref[section, at, :], 1, 1).astype(out_ref.dtype)


def backward(device, step, slopes, blocks, dtype):
    out = jax.ShapeDtypeStruct((slopes.shape[0], blocks.shape[1]), dtype)
    flops = 2 * slopes.size * blocks.shape[1]
    kernel = functools.partial(backward_kernel, step)
    return call(kernel, [out], (device, slopes, blocks), flops, 6, (), [SMEM, VMEM, VMEM])[0]


def gelu_and_slope(value, upstream):
    base = 0.7978845608028654
    cubic = 0.044715
    square = value * value
    s = 0.5 + 0.5 * jnp.tanh(value * (base + (base * cubic) * square))
    act = value * s
    slope = s + (act - act * s) * (2 * base + (6 * base * cubic) * square)
    return act, upstream * slope


def middle_kernel(
    step, chips, device_ref, pre_ref, x_ref, b_ref, low_ref, got_ref, right_ref, up_ref,
    act_ref, slope_ref, mixed_ref, mixed_sent_ref, keep_ref, send_ref, turned_ref, order_ref,
):
    rank = low_ref.shape[1]
    half = rank // 2
    piece = half // chips
    device = device_ref[0]
    total = low_ref[...] + got_ref[...].astype(jnp.float32)
    low = total.astype(jnp.bfloat16)
    turned_ref[...] = low.astype(jnp.float32).T
    for side in range(2):
        for other in range(chips):
            source = ((device & 1) ^ side) * half + chip_at(device, side, chips, other) * piece
            target = side * half + other * piece
            order_ref[target : target + piece, :] = turned_ref[
                pl.ds(pl.multiple_of(source, piece), piece), :
            ].astype(jnp.bfloat16)
    section = section_at(device, step, b_ref.shape[0] - 1)
    x = x_ref[...]
    order = order_ref[...]
    mixed = None
    for at in tiles(up_ref.shape[1], 1024):
        right = right_ref[:, at]
        value = pre_ref[:, at] + dot(x, b_ref[section, :, at], 1, 0) + dot(low, right, 1, 0)
        act, slope = gelu_and_slope(value, up_ref[:, at].astype(jnp.float32))
        act_ref[:, at] = act.astype(jnp.bfloat16)
        slope = slope.astype(jnp.bfloat16)
        slope_ref[:, at] = slope
        part = dot(slope, right, 1, 1)
        mixed = part if mixed is None else mixed + part
        product = dot(order, slope, 1, 0)
        keep_ref[:, at] = product[:half]
        send_ref[:, at] = product[half:].astype(jnp.bfloat16)
    mixed_ref[...] = mixed
    mixed_sent_ref[...] = mixed.astype(jnp.bfloat16)


def middle(device, step, chips, running, x, blocks, low, got, right_factor, upstream):
    rows, cols = upstream.shape
    rank = low.shape[1]
    bf16, f32 = jnp.bfloat16, jnp.float32
    outs = [
        jax.ShapeDtypeStruct((rows, cols), bf16),
        jax.ShapeDtypeStruct((rows, cols), bf16),
        jax.ShapeDtypeStruct((rows, rank), f32),
        jax.ShapeDtypeStruct((rows, rank), bf16),
        jax.ShapeDtypeStruct((rank // 2, cols), f32),
        jax.ShapeDtypeStruct((rank // 2, cols), bf16),
    ]
    args = (device, running, x, blocks, low, got, right_factor, upstream)
    flops = 2 * rows * cols * (x.shape[1] + 3 * rank)
    scratch = [pltpu.VMEM((rank, rows), f32), pltpu.VMEM((rank, rows), bf16)]
    kernel = functools.partial(middle_kernel, step, chips)
    specs = [SMEM] + [VMEM] * (len(args) - 1)
    return call(kernel, outs, args, flops, 16, scratch, specs)


def turn_kernel(*refs):
    out_ref = refs[-1]
    column = 0
    for ref in refs[:-1]:
        rows = ref.shape[0]
        out_ref[:, column : column + rows] = ref[...].astype(jnp.float32).T.astype(jnp.bfloat16)
        column += rows


def turn(parts):
    rows = sum(part.shape[0] for part in parts)
    out = jax.ShapeDtypeStruct((parts[0].shape[1], rows), jnp.bfloat16)
    return call(turn_kernel, [out], parts, 0, 8)[0]


def left_kernel(scale, turned_ref, *refs):
    total_ref, sent_ref = refs[-2:]
    total = None
    column = 0
    for ref in refs[:-2]:
        rows = ref.shape[0]
        part = dot(turned_ref[:, column : column + rows], ref[...], 1, 0)
        total = part if total is None else total + part
        column += rows
    total = total * scale
    total_ref[...] = total
    sent_ref[...] = total.astype(jnp.bfloat16)


def left_partial(turned, mixed, scale):
    shape = (turned.shape[0], mixed[0].shape[1])
    outs = [jax.ShapeDtypeStruct(shape, jnp.float32), jax.ShapeDtypeStruct(shape, jnp.bfloat16)]
    flops = 2 * turned.size * shape[1]
    return call(functools.partial(left_kernel, scale), outs, (turned, *mixed), flops, 6)


def join_kernel(chips, device_ref, *refs):
    parts, out_ref, sem = refs[:-2], refs[-2], refs[-1]
    height = out_ref.shape[0] // (2 * chips)
    device = device_ref[0]
    copies = []
    for side in range(2):
        other = 0
        for ref in parts[side * len(parts) // 2 : (side + 1) * len(parts) // 2]:
            for at in tiles(ref.shape[0], height):
                row = ((device & 1) ^ side) * chips + chip_at(device, side, chips, other)
                target = out_ref.at[pl.ds(pl.multiple_of(row * height, height), height), :]
                copies.append(pltpu.make_async_copy(ref.at[at, :], target, sem.at[len(copies)]))
                other += 1
    for copy in copies:
        copy.start()
    for copy in copies:
        copy.wait()


def join(device, chips, parts):
    out = jax.ShapeDtypeStruct(
        (sum(part.shape[0] for part in parts), parts[0].shape[1]), jnp.bfloat16
    )
    specs = [SMEM] + [VMEM] * len(parts)
    scratch = [pltpu.SemaphoreType.DMA((2 * chips,))]
    kernel = functools.partial(join_kernel, chips)
    return call(kernel, [out], (device, *parts), 0, 2, scratch, specs, [HBM])[0]


def body(tokens, blocks, left_factor, right_factor, upstream):
    bf16, f32 = jnp.bfloat16, jnp.float32
    levels = blocks.shape[0] - 1
    group = lax.axis_size("dp")
    chips = group // 2
    steps = chips.bit_length() - 1
    norm_scale = 1.0 / float(tokens.shape[0] * group) ** 0.5
    device = lax.axis_index("dp").astype(jnp.int32).reshape(1)

    low, low_sent = low_partial(device, tokens, left_factor)
    partners = []
    for step in range(levels):
        got = swap_tensor(low_sent, step, levels)
        partners.append(swap_tensor(tokens, step, levels))
        if step < levels - 1:
            low, low_sent = add(low, got)
    running, held = first(device, tokens, blocks)
    token_parts = [tokens]
    for step in reversed(range(steps)):
        sent = jnp.concatenate(token_parts) if len(token_parts) > 1 else tokens
        token_parts.append(swap_chips(sent, step, steps))
    for step in range(levels - 1):
        running = forward(device, step, partners[step], held, running)
    activated, slopes, mixed, mixed_sent, keep, send = middle(
        device, levels - 1, chips, running, partners[-1], held, low, got, right_factor, upstream
    )
    turned = turn(token_parts)

    mine = keep + swap_core(send).astype(f32)
    for step in range(steps):
        half = mine.shape[0] // 2
        got = swap_chips(mine[half:].astype(bf16), step, steps)
        mine = mine[:half] + got.astype(f32)
    pieces = [(mine * norm_scale).astype(bf16)]

    returned = []
    for step in range(levels):
        got = swap_tensor(mixed_sent, step, levels)
        mixed, mixed_sent = add(mixed, got)
        part = backward(device, step, slopes, held, bf16)
        returned.append(swap_tensor(part, step, levels))
    token_sum = backward(device, None, slopes, held, f32)

    rows_parts = [mixed_sent]
    for step in reversed(range(steps)):
        sent = jnp.concatenate(pieces) if len(pieces) > 1 else pieces[0]
        pieces.append(swap_chips(sent, step, steps))
        sent = jnp.concatenate(rows_parts) if len(rows_parts) > 1 else mixed_sent
        rows_parts.append(swap_chips(sent, step, steps))
    left_total, left_sent = left_partial(turned, rows_parts, norm_scale)
    left_grad = (left_total + swap_core(left_sent).astype(f32)).astype(bf16)
    pieces += [swap_core(part) for part in pieces]
    right_grad = join(device, chips, pieces)

    token_sum = token_sum + dot(mixed_sent, left_factor, 1, 1)
    for part in returned:
        token_sum = token_sum + part.astype(f32)
    return activated, token_sum.astype(bf16), left_grad, right_grad


def solution(mesh):
    placed = (
        P("dp", "tensor"),
        P(None, "tensor", None),
        P("tensor", None),
        P(None, "tensor"),
        P("dp", "tensor"),
    )

    return jax.shard_map(
        body,
        mesh=mesh,
        in_specs=placed,
        out_specs=(P("dp", "tensor"), P("dp", "tensor"), P("tensor", None), P(None, "tensor")),
        check_vma=False,
    )
```

```python
import functools

import jax
import jax.numpy as jnp
from jax import lax
from jax.experimental import pallas as pl
from jax.experimental.pallas import tpu as pltpu
from jax.sharding import PartitionSpec as P


VMEM = pl.BlockSpec(memory_space=pltpu.VMEM)
SMEM = pl.BlockSpec(memory_space=pltpu.SMEM)
HBM = pl.BlockSpec(memory_space=pltpu.HBM)
MIB = 1 << 20


def swap(block, axes, partner):
    dp, tensor = lax.axis_size("dp"), lax.axis_size("tensor")
    if axes == "dp":
        route = [(i, partner(i, 0)) for i in range(dp)]
    else:
        axes = ("dp", "tensor")
        route = [(i * tensor + j, i * tensor + partner(i, j)) for i in range(dp) for j in range(tensor)]
    return lax.ppermute(block, axes, route)


def swap_tensor(block, step, levels):
    return swap(block, "tensor", lambda i, j: j ^ (1 << (levels - 1 - step if i & 1 else step)))


def swap_chips(block, step, count):
    return swap(block, "dp", lambda i, j: i ^ (2 << (count - 1 - step if i & 1 else step)))


def swap_core(block):
    return swap(block, "dp", lambda i, j: i ^ 1)


def dot(left, right, left_dim, right_dim):
    return lax.dot_general(
        left, right, (((left_dim,), (right_dim,)), ((), ())), preferred_element_type=jnp.float32
    )


def tiles(extent, width):
    return [slice(at, min(at + width, extent)) for at in range(0, extent, width)]


def call(kernel, outs, args, flops, mib, scratch=(), in_specs=None, out_specs=None):
    nbytes = sum(a.size * a.dtype.itemsize for a in (*args, *outs))
    return pl.pallas_call(
        kernel,
        out_shape=outs,
        in_specs=in_specs or [VMEM] * len(args),
        out_specs=out_specs or [VMEM] * len(outs),
        scratch_shapes=list(scratch),
        compiler_params=pltpu.CompilerParams(vmem_limit_bytes=mib * MIB),
        cost_estimate=pl.CostEstimate(flops=flops, bytes_accessed=nbytes // 8, transcendentals=0),
    )(*args)


def chip_at(device, side, chips, position):
    steps = chips.bit_length() - 1
    core = (device & 1) ^ side
    up = down = 0
    for step in range(steps):
        if position >> (steps - 1 - step) & 1:
            up |= 1 << step
            down |= 1 << (steps - 1 - step)
    return (device >> 1) ^ (up + core * (down - up))


def section_at(device, step, levels):
    return step + 1 + (device & 1) * (levels - 1 - 2 * step)


def gather_chips(part, count):
    parts = [part]
    for step in reversed(range(count)):
        parts += [swap_chips(held, step, count) for held in parts]
    return parts


def low_kernel(device_ref, x_ref, left_ref, total_ref, sent_ref):
    value = dot(x_ref[...], left_ref[...], 1, 0)
    total_ref[...] = value
    sent_ref[...] = value.astype(jnp.bfloat16)


def low_partial(device, tokens, left_factor):
    shape = (tokens.shape[0], left_factor.shape[1])
    outs = [jax.ShapeDtypeStruct(shape, jnp.float32), jax.ShapeDtypeStruct(shape, jnp.bfloat16)]
    flops = 2 * tokens.size * shape[1]
    specs = [SMEM, VMEM, VMEM]
    return call(low_kernel, outs, (device, tokens, left_factor), flops, 4, (), specs)


def add_kernel(value_ref, got_ref, *outs):
    value = value_ref[...] + got_ref[...].astype(jnp.float32)
    for out_ref in outs:
        out_ref[...] = value.astype(out_ref.dtype)


def add(value, got, dtypes=(jnp.float32, jnp.bfloat16)):
    outs = [jax.ShapeDtypeStruct(value.shape, dtype) for dtype in dtypes]
    return call(add_kernel, outs, (value, got), 0, 2)


def first_kernel(device_ref, x_ref, b_ref, out_ref, held_ref, sem):
    copies = []
    columns = tiles(out_ref.shape[1], 512)
    for index, at in enumerate(columns):
        copies.append(
            pltpu.make_async_copy(b_ref.at[0, :, at], held_ref.at[0, :, at], sem.at[index])
        )
    for section in range(1, b_ref.shape[0]):
        copies.append(
            pltpu.make_async_copy(
                b_ref.at[section], held_ref.at[section], sem.at[len(columns) + section - 1]
            )
        )
    for copy in copies:
        copy.start()
    x = x_ref[...]
    for copy, at in zip(copies, columns):
        copy.wait()
        out_ref[:, at] = dot(x, held_ref[0, :, at], 1, 0)
    for copy in copies[len(columns) :]:
        copy.wait()


def first(device, tokens, blocks):
    outs = [
        jax.ShapeDtypeStruct((tokens.shape[0], blocks.shape[2]), jnp.float32),
        jax.ShapeDtypeStruct(blocks.shape, blocks.dtype),
    ]
    count = len(tiles(blocks.shape[2], 512)) + blocks.shape[0] - 1
    scratch = [pltpu.SemaphoreType.DMA((count,))]
    flops = 2 * tokens.size * blocks.shape[2]
    return call(first_kernel, outs, (device, tokens, blocks), flops, 34, scratch, [SMEM, VMEM, HBM])


def forward_kernel(step, device_ref, b_ref, running_ref, *refs):
    out_ref = refs[-1]
    section = section_at(device_ref[0], step, b_ref.shape[0] - 1)
    x = rows_joined(refs[:-1])
    for at in tiles(out_ref.shape[1], 512):
        out_ref[:, at] = running_ref[:, at] + dot(x, b_ref[section, :, at], 1, 0)


def rows_joined(refs):
    return refs[0][...] if len(refs) == 1 else jnp.concatenate([ref[...] for ref in refs])


def forward(device, step, parts, blocks, running):
    out = jax.ShapeDtypeStruct(running.shape, jnp.float32)
    flops = 2 * running.size * blocks.shape[1]
    kernel = functools.partial(forward_kernel, step)
    args = (device, blocks, running, *parts)
    specs = [SMEM] + [VMEM] * (len(args) - 1)
    return call(kernel, [out], args, flops, 4, (), specs)[0]


def backward_kernel(step, device_ref, s_ref, b_ref, *outs):
    section = 0 if step is None else section_at(device_ref[0], step, b_ref.shape[0] - 1)
    slopes = s_ref[...]
    height = outs[0].shape[0]
    for at in tiles(b_ref.shape[1], 256):
        value = dot(slopes, b_ref[section, at, :], 1, 1)
        for index, out_ref in enumerate(outs):
            rows = value[index * height : (index + 1) * height]
            out_ref[:, at] = rows.astype(out_ref.dtype)


def backward(device, step, slopes, blocks, dtype, count):
    shape = (slopes.shape[0] // count, blocks.shape[1])
    outs = [jax.ShapeDtypeStruct(shape, dtype)] * count
    flops = 2 * slopes.size * blocks.shape[1]
    kernel = functools.partial(backward_kernel, step)
    return call(kernel, outs, (device, slopes, blocks), flops, 6, (), [SMEM, VMEM, VMEM])


def gelu_and_slope(value, upstream):
    base = 0.7978845608028654
    cubic = 0.044715
    square = value * value
    s = 0.5 + 0.5 * jnp.tanh(value * (base + (base * cubic) * square))
    act = value * s
    slope = s + (act - act * s) * (2 * base + (6 * base * cubic) * square)
    return act, upstream * slope


def middle_kernel(
    step, chips, device_ref, pre_ref, x_ref, b_ref, low_ref, got_ref, right_ref, up_ref,
    act_ref, slope_ref, mixed_ref, mixed_sent_ref, keep_ref, send_ref, turned_ref, order_ref,
):
    rank = low_ref.shape[1]
    half = rank // 2
    piece = half // chips
    device = device_ref[0]
    total = low_ref[...] + got_ref[...].astype(jnp.float32)
    low = total.astype(jnp.bfloat16)
    turned_ref[...] = low.astype(jnp.float32).T
    for side in range(2):
        for other in range(chips):
            source = ((device & 1) ^ side) * half + chip_at(device, side, chips, other) * piece
            target = side * half + other * piece
            order_ref[target : target + piece, :] = turned_ref[
                pl.ds(pl.multiple_of(source, piece), piece), :
            ].astype(jnp.bfloat16)
    section = section_at(device, step, b_ref.shape[0] - 1)
    x = x_ref[...]
    order = order_ref[...]
    mixed = None
    for at in tiles(up_ref.shape[1], 1024):
        right = right_ref[:, at]
        value = pre_ref[:, at] + dot(x, b_ref[section, :, at], 1, 0) + dot(low, right, 1, 0)
        act, slope = gelu_and_slope(value, up_ref[:, at].astype(jnp.float32))
        act_ref[:, at] = act.astype(jnp.bfloat16)
        slope = slope.astype(jnp.bfloat16)
        slope_ref[:, at] = slope
        part = dot(slope, right, 1, 1)
        mixed = part if mixed is None else mixed + part
        product = dot(order, slope, 1, 0)
        keep_ref[:, at] = product[:half]
        send_ref[:, at] = product[half:].astype(jnp.bfloat16)
    mixed_ref[...] = mixed
    mixed_sent_ref[...] = mixed.astype(jnp.bfloat16)


def middle(device, step, chips, running, x, blocks, low, got, right_factor, upstream):
    rows, cols = upstream.shape
    rank = low.shape[1]
    bf16, f32 = jnp.bfloat16, jnp.float32
    outs = [
        jax.ShapeDtypeStruct((rows, cols), bf16),
        jax.ShapeDtypeStruct((rows, cols), bf16),
        jax.ShapeDtypeStruct((rows, rank), f32),
        jax.ShapeDtypeStruct((rows, rank), bf16),
        jax.ShapeDtypeStruct((rank // 2, cols), f32),
        jax.ShapeDtypeStruct((rank // 2, cols), bf16),
    ]
    args = (device, running, x, blocks, low, got, right_factor, upstream)
    flops = 2 * rows * cols * (x.shape[1] + 3 * rank)
    scratch = [pltpu.VMEM((rank, rows), f32), pltpu.VMEM((rank, rows), bf16)]
    kernel = functools.partial(middle_kernel, step, chips)
    specs = [SMEM] + [VMEM] * (len(args) - 1)
    return call(kernel, outs, args, flops, 16, scratch, specs)


def turn_kernel(*refs):
    out_ref = refs[-1]
    column = 0
    for ref in refs[:-1]:
        rows = ref.shape[0]
        out_ref[:, column : column + rows] = ref[...].astype(jnp.float32).T.astype(jnp.bfloat16)
        column += rows


def turn(parts):
    rows = sum(part.shape[0] for part in parts)
    out = jax.ShapeDtypeStruct((parts[0].shape[1], rows), jnp.bfloat16)
    return call(turn_kernel, [out], parts, 0, 8)[0]


def left_kernel(scale, early_ref, late_ref, *refs):
    total_ref, sent_ref = refs[-2:]
    total = None
    column = 0
    for ref in refs[:-2]:
        rows = ref.shape[0]
        if column < early_ref.shape[1]:
            turned = early_ref[:, column : column + rows]
        else:
            turned = late_ref[...]
        part = dot(turned, ref[...], 1, 0)
        total = part if total is None else total + part
        column += rows
    total = total * scale
    total_ref[...] = total
    sent_ref[...] = total.astype(jnp.bfloat16)


def left_partial(early, late, mixed, scale):
    shape = (early.shape[0], mixed[0].shape[1])
    outs = [jax.ShapeDtypeStruct(shape, jnp.float32), jax.ShapeDtypeStruct(shape, jnp.bfloat16)]
    flops = 2 * (early.size + late.size) * shape[1]
    kernel = functools.partial(left_kernel, scale)
    return call(kernel, outs, (early, late, *mixed), flops, 6)


def token_kernel(own_ref, mixed_ref, left_ref, *refs):
    returned, out_ref, held_ref, sem = refs[:-3], refs[-3], refs[-2], refs[-1]
    total = own_ref[...] + dot(mixed_ref[...], left_ref[...], 1, 1)
    for index in range(0, len(returned), 2):
        total = total + rows_joined(returned[index : index + 2]).astype(jnp.float32)
    held_ref[...] = total.astype(jnp.bfloat16)
    copy = pltpu.make_async_copy(held_ref, out_ref, sem)
    copy.start()
    copy.wait()


def token_total(own, mixed, left_factor, returned):
    out = jax.ShapeDtypeStruct(own.shape, jnp.bfloat16)
    args = (own, mixed, left_factor, *returned)
    scratch = [pltpu.VMEM(own.shape, jnp.bfloat16), pltpu.SemaphoreType.DMA]
    flops = 2 * own.size * mixed.shape[1]
    return call(token_kernel, [out], args, flops, 4, scratch, None, [HBM])[0]


def finish_kernel(chips, device_ref, total_ref, got_ref, *refs):
    parts = refs[:-4]
    right_ref, left_ref, held_ref, sem = refs[-4:]
    height = right_ref.shape[0] // (2 * chips)
    device = device_ref[0]
    copies = []
    for side in range(2):
        other = 0
        for ref in parts[side * len(parts) // 2 : (side + 1) * len(parts) // 2]:
            for at in tiles(ref.shape[0], height):
                row = ((device & 1) ^ side) * chips + chip_at(device, side, chips, other)
                target = right_ref.at[pl.ds(pl.multiple_of(row * height, height), height), :]
                copies.append(pltpu.make_async_copy(ref.at[at, :], target, sem.at[len(copies)]))
                other += 1
    for copy in copies:
        copy.start()
    held_ref[...] = (total_ref[...] + got_ref[...].astype(jnp.float32)).astype(jnp.bfloat16)
    copies.append(pltpu.make_async_copy(held_ref, left_ref, sem.at[len(copies)]))
    copies[-1].start()
    for copy in copies:
        copy.wait()


def finish(device, chips, left_total, left_got, parts):
    rows = sum(part.shape[0] for part in parts)
    outs = [
        jax.ShapeDtypeStruct((rows, parts[0].shape[1]), jnp.bfloat16),
        jax.ShapeDtypeStruct(left_total.shape, jnp.bfloat16),
    ]
    specs = [SMEM] + [VMEM] * (len(parts) + 2)
    scratch = [
        pltpu.VMEM(left_total.shape, jnp.bfloat16),
        pltpu.SemaphoreType.DMA((2 * chips + 1,)),
    ]
    kernel = functools.partial(finish_kernel, chips)
    args = (device, left_total, left_got, *parts)
    return call(kernel, outs, args, 0, 2, scratch, specs, [HBM, HBM])


def body(tokens, blocks, left_factor, right_factor, upstream):
    bf16, f32 = jnp.bfloat16, jnp.float32
    levels = blocks.shape[0] - 1
    group = lax.axis_size("dp")
    chips = group // 2
    steps = chips.bit_length() - 1
    norm_scale = 1.0 / float(tokens.shape[0] * group) ** 0.5
    device = lax.axis_index("dp").astype(jnp.int32).reshape(1)

    partners = [swap_tensor(tokens, step, levels) for step in range(levels)]
    low, low_sent = low_partial(device, tokens, left_factor)
    for step in range(levels):
        got = swap_tensor(low_sent, step, levels)
        if step < levels - 1:
            low, low_sent = add(low, got)
    running, held = first(device, tokens, blocks)
    token_parts = gather_chips(tokens, steps)
    for step in range(levels - 1):
        running = forward(device, step, [partners[step]], held, running)
    activated, slopes, mixed, mixed_sent, keep, send = middle(
        device, levels - 1, chips, running, partners[-1], held, low, got, right_factor, upstream
    )
    early, late = turn(token_parts[:-1]), turn(token_parts[-1:])

    mine = keep + swap_core(send).astype(f32)
    for step in range(steps):
        half = mine.shape[0] // 2
        got = swap_chips(mine[half:].astype(bf16), step, steps)
        mine = mine[:half] + got.astype(f32)
    piece = (mine * norm_scale).astype(bf16)

    returned = []
    for step in range(levels):
        got = swap_tensor(mixed_sent, step, levels)
        if step < levels - 1:
            mixed, mixed_sent = add(mixed, got)
        else:
            mixed_rows = add(mixed, got, (bf16,))[0]
        parts = backward(device, step, slopes, held, bf16, 2)
        returned += [swap_tensor(part, step, levels) for part in parts]
    own = backward(device, None, slopes, held, f32, 1)[0]

    pieces = gather_chips(piece, steps)
    rows_parts = gather_chips(mixed_rows, steps)
    left_total, left_sent = left_partial(early, late, rows_parts, norm_scale)
    left_got = swap_core(left_sent)
    pieces += [swap_core(part) for part in pieces]
    right_grad, left_grad = finish(device, chips, left_total, left_got, pieces)
    token_grad = token_total(own, mixed_rows, left_factor, returned)
    return activated, token_grad, left_grad, right_grad


def solution(mesh):
    placed = (
        P("dp", "tensor"),
        P(None, "tensor", None),
        P("tensor", None),
        P(None, "tensor"),
        P("dp", "tensor"),
    )

    return jax.shard_map(
        body,
        mesh=mesh,
        in_specs=placed,
        out_specs=(P("dp", "tensor"), P("dp", "tensor"), P("tensor", None), P(None, "tensor")),
        check_vma=False,
    )
```

```python
import functools

import jax
import jax.numpy as jnp
from jax import lax
from jax.experimental import pallas as pl
from jax.experimental.pallas import tpu as pltpu
from jax.sharding import PartitionSpec as P


VMEM = pl.BlockSpec(memory_space=pltpu.VMEM)
SMEM = pl.BlockSpec(memory_space=pltpu.SMEM)
HBM = pl.BlockSpec(memory_space=pltpu.HBM)
MIB = 1 << 20


def swap(block, axes, partner):
    dp, tensor = lax.axis_size("dp"), lax.axis_size("tensor")
    if axes == "dp":
        route = [(i, partner(i, 0)) for i in range(dp)]
    else:
        axes = ("dp", "tensor")
        route = [(i * tensor + j, i * tensor + partner(i, j)) for i in range(dp) for j in range(tensor)]
    return lax.ppermute(block, axes, route)


def swap_tensor(block, step, levels):
    return swap(block, "tensor", lambda i, j: j ^ (1 << (levels - 1 - step if i & 1 else step)))


def swap_chips(block, step, count):
    return swap(block, "dp", lambda i, j: i ^ (2 << (count - 1 - step if i & 1 else step)))


def swap_core(block):
    return swap(block, "dp", lambda i, j: i ^ 1)


def dot(left, right, left_dim, right_dim):
    return lax.dot_general(
        left, right, (((left_dim,), (right_dim,)), ((), ())), preferred_element_type=jnp.float32
    )


def tiles(extent, width):
    return [slice(at, min(at + width, extent)) for at in range(0, extent, width)]


def call(kernel, outs, args, flops, mib, scratch=(), in_specs=None, out_specs=None):
    nbytes = sum(a.size * a.dtype.itemsize for a in (*args, *outs))
    return pl.pallas_call(
        kernel,
        out_shape=outs,
        in_specs=in_specs or [VMEM] * len(args),
        out_specs=out_specs or [VMEM] * len(outs),
        scratch_shapes=list(scratch),
        compiler_params=pltpu.CompilerParams(vmem_limit_bytes=mib * MIB),
        cost_estimate=pl.CostEstimate(flops=flops, bytes_accessed=nbytes // 8, transcendentals=0),
    )(*args)


def chip_at(device, side, chips, position):
    steps = chips.bit_length() - 1
    core = (device & 1) ^ side
    up = down = 0
    for step in range(steps):
        if position >> (steps - 1 - step) & 1:
            up |= 1 << step
            down |= 1 << (steps - 1 - step)
    return (device >> 1) ^ (up + core * (down - up))


def section_at(device, step, levels):
    return step + 1 + (device & 1) * (levels - 1 - 2 * step)


def gather_chips(part, count):
    parts = [part]
    for step in reversed(range(count)):
        parts += [swap_chips(held, step, count) for held in parts]
    return parts


def low_kernel(device_ref, x_ref, left_ref, total_ref, sent_ref):
    value = dot(x_ref[...], left_ref[...], 1, 0)
    total_ref[...] = value
    sent_ref[...] = value.astype(jnp.bfloat16)


def low_partial(device, tokens, left_factor):
    shape = (tokens.shape[0], left_factor.shape[1])
    outs = [jax.ShapeDtypeStruct(shape, jnp.float32), jax.ShapeDtypeStruct(shape, jnp.bfloat16)]
    flops = 2 * tokens.size * shape[1]
    specs = [SMEM, VMEM, VMEM]
    return call(low_kernel, outs, (device, tokens, left_factor), flops, 4, (), specs)


def add_kernel(value_ref, got_ref, *outs):
    value = value_ref[...] + got_ref[...].astype(jnp.float32)
    for out_ref in outs:
        out_ref[...] = value.astype(out_ref.dtype)


def add(value, got, dtypes=(jnp.float32, jnp.bfloat16)):
    outs = [jax.ShapeDtypeStruct(value.shape, dtype) for dtype in dtypes]
    return call(add_kernel, outs, (value, got), 0, 2)


def first_kernel(device_ref, x_ref, b_ref, out_ref, held_ref, sem):
    copies = []
    columns = tiles(out_ref.shape[1], 512)
    for index, at in enumerate(columns):
        copies.append(
            pltpu.make_async_copy(b_ref.at[0, :, at], held_ref.at[0, :, at], sem.at[index])
        )
    for section in range(1, b_ref.shape[0]):
        copies.append(
            pltpu.make_async_copy(
                b_ref.at[section], held_ref.at[section], sem.at[len(columns) + section - 1]
            )
        )
    for copy in copies:
        copy.start()
    x = x_ref[...]
    for copy, at in zip(copies, columns):
        copy.wait()
        out_ref[:, at] = dot(x, held_ref[0, :, at], 1, 0)
    for copy in copies[len(columns) :]:
        copy.wait()


def first(device, tokens, blocks):
    outs = [
        jax.ShapeDtypeStruct((tokens.shape[0], blocks.shape[2]), jnp.float32),
        jax.ShapeDtypeStruct(blocks.shape, blocks.dtype),
    ]
    count = len(tiles(blocks.shape[2], 512)) + blocks.shape[0] - 1
    scratch = [pltpu.SemaphoreType.DMA((count,))]
    flops = 2 * tokens.size * blocks.shape[2]
    return call(first_kernel, outs, (device, tokens, blocks), flops, 34, scratch, [SMEM, VMEM, HBM])


def forward_kernel(step, device_ref, b_ref, running_ref, *refs):
    out_ref = refs[-1]
    section = section_at(device_ref[0], step, b_ref.shape[0] - 1)
    x = rows_joined(refs[:-1])
    for at in tiles(out_ref.shape[1], 512):
        out_ref[:, at] = running_ref[:, at] + dot(x, b_ref[section, :, at], 1, 0)


def rows_joined(refs):
    return refs[0][...] if len(refs) == 1 else jnp.concatenate([ref[...] for ref in refs])


def forward(device, step, parts, blocks, running):
    out = jax.ShapeDtypeStruct(running.shape, jnp.float32)
    flops = 2 * running.size * blocks.shape[1]
    kernel = functools.partial(forward_kernel, step)
    args = (device, blocks, running, *parts)
    specs = [SMEM] + [VMEM] * (len(args) - 1)
    return call(kernel, [out], args, flops, 4, (), specs)[0]


def backward_kernel(step, device_ref, s_ref, b_ref, *outs):
    section = 0 if step is None else section_at(device_ref[0], step, b_ref.shape[0] - 1)
    slopes = s_ref[...]
    height = outs[0].shape[0]
    for at in tiles(b_ref.shape[1], 256):
        value = dot(slopes, b_ref[section, at, :], 1, 1)
        for index, out_ref in enumerate(outs):
            rows = value[index * height : (index + 1) * height]
            out_ref[:, at] = rows.astype(out_ref.dtype)


def backward(device, step, slopes, blocks, dtype, count):
    shape = (slopes.shape[0] // count, blocks.shape[1])
    outs = [jax.ShapeDtypeStruct(shape, dtype)] * count
    flops = 2 * slopes.size * blocks.shape[1]
    kernel = functools.partial(backward_kernel, step)
    return call(kernel, outs, (device, slopes, blocks), flops, 6, (), [SMEM, VMEM, VMEM])


def gelu_and_slope(value, upstream):
    base = 0.7978845608028654
    cubic = 0.044715
    square = value * value
    s = 0.5 + 0.5 * jnp.tanh(value * (base + (base * cubic) * square))
    act = value * s
    slope = s + (act - act * s) * (2 * base + (6 * base * cubic) * square)
    return act, upstream * slope


def middle_kernel(
    chips, device_ref, pre_ref, low_ref, got_ref, right_ref, up_ref,
    act_ref, slope_ref, mixed_ref, mixed_sent_ref, keep_ref, send_ref, turned_ref, order_ref,
):
    rank = low_ref.shape[1]
    half = rank // 2
    piece = half // chips
    device = device_ref[0]
    total = low_ref[...] + got_ref[...].astype(jnp.float32)
    low = total.astype(jnp.bfloat16)
    turned_ref[...] = low.astype(jnp.float32).T
    for side in range(2):
        for other in range(chips):
            source = ((device & 1) ^ side) * half + chip_at(device, side, chips, other) * piece
            target = side * half + other * piece
            order_ref[target : target + piece, :] = turned_ref[
                pl.ds(pl.multiple_of(source, piece), piece), :
            ].astype(jnp.bfloat16)
    order = order_ref[...]
    mixed = None
    for at in tiles(up_ref.shape[1], 1024):
        right = right_ref[:, at]
        value = pre_ref[:, at] + dot(low, right, 1, 0)
        act, slope = gelu_and_slope(value, up_ref[:, at].astype(jnp.float32))
        act_ref[:, at] = act.astype(jnp.bfloat16)
        slope = slope.astype(jnp.bfloat16)
        slope_ref[:, at] = slope
        part = dot(slope, right, 1, 1)
        mixed = part if mixed is None else mixed + part
        product = dot(order, slope, 1, 0)
        keep_ref[:, at] = product[:half]
        send_ref[:, at] = product[half:].astype(jnp.bfloat16)
    mixed_ref[...] = mixed
    mixed_sent_ref[...] = mixed.astype(jnp.bfloat16)


def middle(device, chips, running, low, got, right_factor, upstream):
    rows, cols = upstream.shape
    rank = low.shape[1]
    bf16, f32 = jnp.bfloat16, jnp.float32
    outs = [
        jax.ShapeDtypeStruct((rows, cols), bf16),
        jax.ShapeDtypeStruct((rows, cols), bf16),
        jax.ShapeDtypeStruct((rows, rank), f32),
        jax.ShapeDtypeStruct((rows, rank), bf16),
        jax.ShapeDtypeStruct((rank // 2, cols), f32),
        jax.ShapeDtypeStruct((rank // 2, cols), bf16),
    ]
    args = (device, running, low, got, right_factor, upstream)
    flops = 2 * rows * cols * 3 * rank
    scratch = [pltpu.VMEM((rank, rows), f32), pltpu.VMEM((rank, rows), bf16)]
    kernel = functools.partial(middle_kernel, chips)
    specs = [SMEM] + [VMEM] * (len(args) - 1)
    return call(kernel, outs, args, flops, 16, scratch, specs)


def turn_kernel(*refs):
    out_ref = refs[-1]
    column = 0
    for ref in refs[:-1]:
        rows = ref.shape[0]
        out_ref[:, column : column + rows] = ref[...].astype(jnp.float32).T.astype(jnp.bfloat16)
        column += rows


def turn(parts):
    rows = sum(part.shape[0] for part in parts)
    out = jax.ShapeDtypeStruct((parts[0].shape[1], rows), jnp.bfloat16)
    return call(turn_kernel, [out], parts, 0, 8)[0]


def left_kernel(scale, early_ref, late_ref, *refs):
    total_ref, sent_ref = refs[-2:]
    total = None
    column = 0
    for ref in refs[:-2]:
        rows = ref.shape[0]
        if column < early_ref.shape[1]:
            turned = early_ref[:, column : column + rows]
        else:
            turned = late_ref[...]
        part = dot(turned, ref[...], 1, 0)
        total = part if total is None else total + part
        column += rows
    total = total * scale
    total_ref[...] = total
    sent_ref[...] = total.astype(jnp.bfloat16)


def left_partial(early, late, mixed, scale):
    shape = (early.shape[0], mixed[0].shape[1])
    outs = [jax.ShapeDtypeStruct(shape, jnp.float32), jax.ShapeDtypeStruct(shape, jnp.bfloat16)]
    flops = 2 * (early.size + late.size) * shape[1]
    kernel = functools.partial(left_kernel, scale)
    return call(kernel, outs, (early, late, *mixed), flops, 6)


def token_kernel(counts, own_ref, mixed_ref, left_ref, *refs):
    returned, out_ref, held_ref, sem = refs[:-3], refs[-3], refs[-2], refs[-1]
    total = own_ref[...] + dot(mixed_ref[...], left_ref[...], 1, 1)
    for count in counts:
        total = total + rows_joined(returned[:count]).astype(jnp.float32)
        returned = returned[count:]
    held_ref[...] = total.astype(jnp.bfloat16)
    copy = pltpu.make_async_copy(held_ref, out_ref, sem)
    copy.start()
    copy.wait()


def token_total(own, mixed, left_factor, returned):
    out = jax.ShapeDtypeStruct(own.shape, jnp.bfloat16)
    args = (own, mixed, left_factor, *(part for parts in returned for part in parts))
    kernel = functools.partial(token_kernel, [len(parts) for parts in returned])
    scratch = [pltpu.VMEM(own.shape, jnp.bfloat16), pltpu.SemaphoreType.DMA]
    flops = 2 * own.size * mixed.shape[1]
    return call(kernel, [out], args, flops, 4, scratch, None, [HBM])[0]


def finish_kernel(chips, device_ref, total_ref, got_ref, *refs):
    parts = refs[:-4]
    right_ref, left_ref, held_ref, sem = refs[-4:]
    height = right_ref.shape[0] // (2 * chips)
    device = device_ref[0]
    copies = []
    for side in range(2):
        other = 0
        for ref in parts[side * len(parts) // 2 : (side + 1) * len(parts) // 2]:
            for at in tiles(ref.shape[0], height):
                row = ((device & 1) ^ side) * chips + chip_at(device, side, chips, other)
                target = right_ref.at[pl.ds(pl.multiple_of(row * height, height), height), :]
                copies.append(pltpu.make_async_copy(ref.at[at, :], target, sem.at[len(copies)]))
                other += 1
    for copy in copies:
        copy.start()
    held_ref[...] = (total_ref[...] + got_ref[...].astype(jnp.float32)).astype(jnp.bfloat16)
    copies.append(pltpu.make_async_copy(held_ref, left_ref, sem.at[len(copies)]))
    copies[-1].start()
    for copy in copies:
        copy.wait()


def finish(device, chips, left_total, left_got, parts):
    rows = sum(part.shape[0] for part in parts)
    outs = [
        jax.ShapeDtypeStruct((rows, parts[0].shape[1]), jnp.bfloat16),
        jax.ShapeDtypeStruct(left_total.shape, jnp.bfloat16),
    ]
    specs = [SMEM] + [VMEM] * (len(parts) + 2)
    scratch = [
        pltpu.VMEM(left_total.shape, jnp.bfloat16),
        pltpu.SemaphoreType.DMA((2 * chips + 1,)),
    ]
    kernel = functools.partial(finish_kernel, chips)
    args = (device, left_total, left_got, *parts)
    return call(kernel, outs, args, 0, 2, scratch, specs, [HBM, HBM])


def body(tokens, blocks, left_factor, right_factor, upstream):
    bf16, f32 = jnp.bfloat16, jnp.float32
    levels = blocks.shape[0] - 1
    group = lax.axis_size("dp")
    chips = group // 2
    steps = chips.bit_length() - 1
    norm_scale = 1.0 / float(tokens.shape[0] * group) ** 0.5
    device = lax.axis_index("dp").astype(jnp.int32).reshape(1)

    partners = [swap_tensor(tokens, step, levels) for step in range(levels)]
    low, low_sent = low_partial(device, tokens, left_factor)
    for step in range(levels):
        got = swap_tensor(low_sent, step, levels)
        if step < levels - 1:
            low, low_sent = add(low, got)
    running, held = first(device, tokens, blocks)
    token_parts = gather_chips(tokens, steps)
    for step in range(levels):
        running = forward(device, step, [partners[step]], held, running)
    activated, slopes, mixed, mixed_sent, keep, send = middle(
        device, chips, running, low, got, right_factor, upstream
    )
    early, late = turn(token_parts[:-1]), turn(token_parts[-1:])

    mine = keep + swap_core(send).astype(f32)
    for step in range(steps):
        half = mine.shape[0] // 2
        got = swap_chips(mine[half:].astype(bf16), step, steps)
        mine = mine[:half] + got.astype(f32)
    piece = (mine * norm_scale).astype(bf16)

    returned = []
    for step in range(levels):
        got = swap_tensor(mixed_sent, step, levels)
        if step < levels - 1:
            mixed, mixed_sent = add(mixed, got)
        else:
            mixed_rows = add(mixed, got, (bf16,))[0]
        count = 1 if step == levels - 1 else 2
        parts = backward(device, step, slopes, held, bf16, count)
        returned.append([swap_tensor(part, step, levels) for part in parts])
    own = backward(device, None, slopes, held, f32, 1)[0]

    pieces = gather_chips(piece, steps)
    rows_parts = gather_chips(mixed_rows, steps)
    left_total, left_sent = left_partial(early, late, rows_parts, norm_scale)
    left_got = swap_core(left_sent)
    pieces += [swap_core(part) for part in pieces]
    right_grad, left_grad = finish(device, chips, left_total, left_got, pieces)
    token_grad = token_total(own, mixed_rows, left_factor, returned)
    return activated, token_grad, left_grad, right_grad


def solution(mesh):
    placed = (
        P("dp", "tensor"),
        P(None, "tensor", None),
        P("tensor", None),
        P(None, "tensor"),
        P("dp", "tensor"),
    )

    return jax.shard_map(
        body,
        mesh=mesh,
        in_specs=placed,
        out_specs=(P("dp", "tensor"), P("dp", "tensor"), P("tensor", None), P(None, "tensor")),
        check_vma=False,
    )
```

```python
import functools

import jax
import jax.numpy as jnp
from jax import lax
from jax.experimental import pallas as pl
from jax.experimental.pallas import tpu as pltpu
from jax.sharding import PartitionSpec as P


VMEM = pl.BlockSpec(memory_space=pltpu.VMEM)
SMEM = pl.BlockSpec(memory_space=pltpu.SMEM)
HBM = pl.BlockSpec(memory_space=pltpu.HBM)
MIB = 1 << 20


def swap(block, axes, partner):
    dp, tensor = lax.axis_size("dp"), lax.axis_size("tensor")
    if axes == "dp":
        route = [(i, partner(i, 0)) for i in range(dp)]
    else:
        axes = ("dp", "tensor")
        route = [(i * tensor + j, i * tensor + partner(i, j)) for i in range(dp) for j in range(tensor)]
    return lax.ppermute(block, axes, route)


def swap_tensor(block, step, levels):
    return swap(block, "tensor", lambda i, j: j ^ (1 << (levels - 1 - step if i & 1 else step)))


def swap_chips(block, step, count):
    return swap(block, "dp", lambda i, j: i ^ (2 << (count - 1 - step if i & 1 else step)))


def swap_core(block):
    return swap(block, "dp", lambda i, j: i ^ 1)


def dot(left, right, left_dim, right_dim):
    return lax.dot_general(
        left, right, (((left_dim,), (right_dim,)), ((), ())), preferred_element_type=jnp.float32
    )


def tiles(extent, width):
    return [slice(at, min(at + width, extent)) for at in range(0, extent, width)]


def call(kernel, outs, args, flops, mib, scratch=(), in_specs=None, out_specs=None, aliases=None):
    nbytes = sum(a.size * a.dtype.itemsize for a in (*args, *outs))
    return pl.pallas_call(
        kernel,
        out_shape=outs,
        in_specs=in_specs or [VMEM] * len(args),
        out_specs=out_specs or [VMEM] * len(outs),
        scratch_shapes=list(scratch),
        input_output_aliases=aliases or {},
        compiler_params=pltpu.CompilerParams(vmem_limit_bytes=mib * MIB),
        cost_estimate=pl.CostEstimate(flops=flops, bytes_accessed=nbytes // 8, transcendentals=0),
    )(*args)


def chip_at(device, side, chips, position):
    steps = chips.bit_length() - 1
    core = (device & 1) ^ side
    up = down = 0
    for step in range(steps):
        if position >> (steps - 1 - step) & 1:
            up |= 1 << step
            down |= 1 << (steps - 1 - step)
    return (device >> 1) ^ (up + core * (down - up))


def section_at(device, step, levels):
    return step + 1 + (device & 1) * (levels - 1 - 2 * step)


def gather_chips(part, count):
    parts = [part]
    for step in reversed(range(count)):
        parts += [swap_chips(held, step, count) for held in parts]
    return parts


def low_kernel(device_ref, x_ref, left_ref, total_ref, sent_ref):
    value = dot(x_ref[...], left_ref[...], 1, 0)
    total_ref[...] = value
    sent_ref[...] = value.astype(jnp.bfloat16)


def low_partial(device, tokens, left_factor):
    shape = (tokens.shape[0], left_factor.shape[1])
    outs = [jax.ShapeDtypeStruct(shape, jnp.float32), jax.ShapeDtypeStruct(shape, jnp.bfloat16)]
    flops = 2 * tokens.size * shape[1]
    specs = [SMEM, VMEM, VMEM]
    return call(low_kernel, outs, (device, tokens, left_factor), flops, 4, (), specs)


def add_kernel(value_ref, got_ref, *outs):
    value = value_ref[...] + got_ref[...].astype(jnp.float32)
    for out_ref in outs:
        out_ref[...] = value.astype(out_ref.dtype)


def add(value, got, dtypes=(jnp.float32, jnp.bfloat16)):
    outs = [jax.ShapeDtypeStruct(value.shape, dtype) for dtype in dtypes]
    return call(add_kernel, outs, (value, got), 0, 2)


def first_kernel(device_ref, x_ref, b_ref, out_ref, held_ref, sem):
    copies = []
    columns = tiles(out_ref.shape[1], 512)
    for index, at in enumerate(columns):
        copies.append(
            pltpu.make_async_copy(b_ref.at[0, :, at], held_ref.at[0, :, at], sem.at[index])
        )
    for section in range(1, b_ref.shape[0]):
        copies.append(
            pltpu.make_async_copy(
                b_ref.at[section], held_ref.at[section], sem.at[len(columns) + section - 1]
            )
        )
    for copy in copies:
        copy.start()
    x = x_ref[...]
    for copy, at in zip(copies, columns):
        copy.wait()
        out_ref[:, at] = dot(x, held_ref[0, :, at], 1, 0)
    for copy in copies[len(columns) :]:
        copy.wait()


def first(device, tokens, blocks):
    outs = [
        jax.ShapeDtypeStruct((tokens.shape[0], blocks.shape[2]), jnp.float32),
        jax.ShapeDtypeStruct(blocks.shape, blocks.dtype),
    ]
    count = len(tiles(blocks.shape[2], 512)) + blocks.shape[0] - 1
    scratch = [pltpu.SemaphoreType.DMA((count,))]
    flops = 2 * tokens.size * blocks.shape[2]
    return call(first_kernel, outs, (device, tokens, blocks), flops, 34, scratch, [SMEM, VMEM, HBM])


def forward_kernel(step, device_ref, b_ref, running_ref, *refs):
    out_ref = refs[-1]
    section = section_at(device_ref[0], step, b_ref.shape[0] - 1)
    x = rows_joined(refs[:-1])
    for at in tiles(out_ref.shape[1], 512):
        out_ref[:, at] = running_ref[:, at] + dot(x, b_ref[section, :, at], 1, 0)


def rows_joined(refs):
    return refs[0][...] if len(refs) == 1 else jnp.concatenate([ref[...] for ref in refs])


def forward(device, step, parts, blocks, running):
    out = jax.ShapeDtypeStruct(running.shape, jnp.float32)
    flops = 2 * running.size * blocks.shape[1]
    kernel = functools.partial(forward_kernel, step)
    args = (device, blocks, running, *parts)
    specs = [SMEM] + [VMEM] * (len(args) - 1)
    return call(kernel, [out], args, flops, 4, (), specs)[0]


def backward_kernel(step, device_ref, s_ref, b_ref, *outs):
    section = 0 if step is None else section_at(device_ref[0], step, b_ref.shape[0] - 1)
    slopes = s_ref[...]
    height = outs[0].shape[0]
    for at in tiles(b_ref.shape[1], 256):
        value = dot(slopes, b_ref[section, at, :], 1, 1)
        for index, out_ref in enumerate(outs):
            rows = value[index * height : (index + 1) * height]
            out_ref[:, at] = rows.astype(out_ref.dtype)


def backward(device, step, slopes, blocks, dtype, count):
    shape = (slopes.shape[0] // count, blocks.shape[1])
    outs = [jax.ShapeDtypeStruct(shape, dtype)] * count
    flops = 2 * slopes.size * blocks.shape[1]
    kernel = functools.partial(backward_kernel, step)
    return call(kernel, outs, (device, slopes, blocks), flops, 6, (), [SMEM, VMEM, VMEM])


def gelu_and_slope(value, upstream):
    base = 0.7978845608028654
    cubic = 0.044715
    square = value * value
    s = 0.5 + 0.5 * jnp.tanh(value * (base + (base * cubic) * square))
    act = value * s
    slope = s + (act - act * s) * (2 * base + (6 * base * cubic) * square)
    return act, upstream * slope


def middle_kernel(
    chips, device_ref, pre_ref, low_ref, got_ref, right_ref, up_ref,
    act_ref, slope_ref, mixed_ref, mixed_sent_ref, keep_ref, send_ref, turned_ref, order_ref,
):
    rank = low_ref.shape[1]
    half = rank // 2
    piece = half // chips
    device = device_ref[0]
    total = low_ref[...] + got_ref[...].astype(jnp.float32)
    low = total.astype(jnp.bfloat16)
    turned_ref[...] = low.astype(jnp.float32).T
    for side in range(2):
        for other in range(chips):
            source = ((device & 1) ^ side) * half + chip_at(device, side, chips, other) * piece
            target = side * half + other * piece
            order_ref[target : target + piece, :] = turned_ref[
                pl.ds(pl.multiple_of(source, piece), piece), :
            ].astype(jnp.bfloat16)
    order = order_ref[...]
    mixed = None
    for at in tiles(up_ref.shape[1], 1536):
        right = right_ref[:, at]
        value = pre_ref[:, at] + dot(low, right, 1, 0)
        act, slope = gelu_and_slope(value, up_ref[:, at].astype(jnp.float32))
        act_ref[:, at] = act.astype(jnp.bfloat16)
        slope = slope.astype(jnp.bfloat16)
        slope_ref[:, at] = slope
        part = dot(slope, right, 1, 1)
        mixed = part if mixed is None else mixed + part
        product = dot(order, slope, 1, 0)
        keep_ref[:, at] = product[:half]
        send_ref[:, at] = product[half:].astype(jnp.bfloat16)
    mixed_ref[...] = mixed
    mixed_sent_ref[...] = mixed.astype(jnp.bfloat16)


def middle(device, chips, running, low, got, right_factor, upstream):
    rows, cols = upstream.shape
    rank = low.shape[1]
    bf16, f32 = jnp.bfloat16, jnp.float32
    outs = [
        jax.ShapeDtypeStruct((rows, cols), bf16),
        jax.ShapeDtypeStruct((rows, cols), bf16),
        jax.ShapeDtypeStruct((rows, rank), f32),
        jax.ShapeDtypeStruct((rows, rank), bf16),
        jax.ShapeDtypeStruct((rank // 2, cols), f32),
        jax.ShapeDtypeStruct((rank // 2, cols), bf16),
    ]
    args = (device, running, low, got, right_factor, upstream)
    flops = 2 * rows * cols * 3 * rank
    scratch = [pltpu.VMEM((rank, rows), f32), pltpu.VMEM((rank, rows), bf16)]
    kernel = functools.partial(middle_kernel, chips)
    specs = [SMEM] + [VMEM] * (len(args) - 1)
    return call(kernel, outs, args, flops, 16, scratch, specs)


def turn_kernel(*refs):
    out_ref = refs[-1]
    column = 0
    for ref in refs[:-1]:
        rows = ref.shape[0]
        out_ref[:, column : column + rows] = ref[...].astype(jnp.float32).T.astype(jnp.bfloat16)
        column += rows


def turn(parts):
    rows = sum(part.shape[0] for part in parts)
    out = jax.ShapeDtypeStruct((parts[0].shape[1], rows), jnp.bfloat16)
    return call(turn_kernel, [out], parts, 0, 8)[0]


def left_kernel(scale, early_ref, late_ref, *refs):
    total_ref, sent_ref = refs[-2:]
    total = None
    column = 0
    for ref in refs[:-2]:
        rows = ref.shape[0]
        if column < early_ref.shape[1]:
            turned = early_ref[:, column : column + rows]
        else:
            turned = late_ref[...]
        part = dot(turned, ref[...], 1, 0)
        total = part if total is None else total + part
        column += rows
    total = total * scale
    total_ref[...] = total
    sent_ref[...] = total.astype(jnp.bfloat16)


def left_partial(early, late, mixed, scale):
    shape = (early.shape[0], mixed[0].shape[1])
    outs = [jax.ShapeDtypeStruct(shape, jnp.float32), jax.ShapeDtypeStruct(shape, jnp.bfloat16)]
    flops = 2 * (early.size + late.size) * shape[1]
    kernel = functools.partial(left_kernel, scale)
    return call(kernel, outs, (early, late, *mixed), flops, 6)


def token_kernel(counts, own_ref, mixed_ref, left_ref, *refs):
    returned, out_ref, held_ref, sem = refs[:-3], refs[-3], refs[-2], refs[-1]
    total = own_ref[...] + dot(mixed_ref[...], left_ref[...], 1, 1)
    for count in counts:
        total = total + rows_joined(returned[:count]).astype(jnp.float32)
        returned = returned[count:]
    held_ref[...] = total.astype(jnp.bfloat16)
    copy = pltpu.make_async_copy(held_ref, out_ref, sem)
    copy.start()
    copy.wait()


def token_total(own, mixed, left_factor, returned):
    out = jax.ShapeDtypeStruct(own.shape, jnp.bfloat16)
    args = (own, mixed, left_factor, *(part for parts in returned for part in parts))
    kernel = functools.partial(token_kernel, [len(parts) for parts in returned])
    scratch = [pltpu.VMEM(own.shape, jnp.bfloat16), pltpu.SemaphoreType.DMA]
    flops = 2 * own.size * mixed.shape[1]
    return call(kernel, [out], args, flops, 4, scratch, None, [HBM])[0]


def place_copies(device, chips, parts, positions, out_ref, sem):
    height = out_ref.shape[0] // (2 * chips)
    copies = []
    for ref, (side, position) in zip(parts, positions):
        row = ((device & 1) ^ side) * chips + chip_at(device, side, chips, position)
        target = out_ref.at[pl.ds(pl.multiple_of(row * height, height), height), :]
        copies.append(pltpu.make_async_copy(ref, target, sem.at[len(copies)]))
    for copy in copies:
        copy.start()
    return copies


def place_kernel(chips, positions, device_ref, *refs):
    parts, out_ref, sem = refs[:-2], refs[-2], refs[-1]
    for copy in place_copies(device_ref[0], chips, parts, positions, out_ref, sem):
        copy.wait()


def place(device, chips, parts, positions):
    height, cols = parts[0].shape
    out = jax.ShapeDtypeStruct((2 * chips * height, cols), jnp.bfloat16)
    specs = [SMEM] + [VMEM] * len(parts)
    scratch = [pltpu.SemaphoreType.DMA((len(parts),))]
    kernel = functools.partial(place_kernel, chips, positions)
    return call(kernel, [out], (device, *parts), 0, 2, scratch, specs, [HBM])[0]


def finish_kernel(chips, positions, device_ref, placed_ref, total_ref, got_ref, *refs):
    parts = refs[:-4]
    right_ref, left_ref, held_ref, sem = refs[-4:]
    copies = place_copies(device_ref[0], chips, parts, positions, right_ref, sem)
    held_ref[...] = (total_ref[...] + got_ref[...].astype(jnp.float32)).astype(jnp.bfloat16)
    copies.append(pltpu.make_async_copy(held_ref, left_ref, sem.at[len(copies)]))
    copies[-1].start()
    for copy in copies:
        copy.wait()


def finish(device, chips, placed, left_total, left_got, parts, positions):
    outs = [
        jax.ShapeDtypeStruct(placed.shape, placed.dtype),
        jax.ShapeDtypeStruct(left_total.shape, jnp.bfloat16),
    ]
    specs = [SMEM, HBM] + [VMEM] * (len(parts) + 2)
    scratch = [
        pltpu.VMEM(left_total.shape, jnp.bfloat16),
        pltpu.SemaphoreType.DMA((len(parts) + 1,)),
    ]
    kernel = functools.partial(finish_kernel, chips, positions)
    args = (device, placed, left_total, left_got, *parts)
    return call(kernel, outs, args, 0, 2, scratch, specs, [HBM, HBM], {1: 0})


def body(tokens, blocks, left_factor, right_factor, upstream):
    bf16, f32 = jnp.bfloat16, jnp.float32
    levels = blocks.shape[0] - 1
    group = lax.axis_size("dp")
    chips = group // 2
    steps = chips.bit_length() - 1
    norm_scale = 1.0 / float(tokens.shape[0] * group) ** 0.5
    device = lax.axis_index("dp").astype(jnp.int32).reshape(1)

    partners = [swap_tensor(tokens, step, levels) for step in range(levels)]
    low, low_sent = low_partial(device, tokens, left_factor)
    for step in range(levels):
        got = swap_tensor(low_sent, step, levels)
        if step < levels - 1:
            low, low_sent = add(low, got)
    running, held = first(device, tokens, blocks)
    token_parts = gather_chips(tokens, steps)
    for step in range(levels):
        running = forward(device, step, [partners[step]], held, running)
    activated, slopes, mixed, mixed_sent, keep, send = middle(
        device, chips, running, low, got, right_factor, upstream
    )
    early, late = turn(token_parts[:-1]), turn(token_parts[-1:])

    mine = keep + swap_core(send).astype(f32)
    for step in range(steps):
        half = mine.shape[0] // 2
        got = swap_chips(mine[half:].astype(bf16), step, steps)
        mine = mine[:half] + got.astype(f32)
    piece = (mine * norm_scale).astype(bf16)

    returned = []
    for step in range(levels):
        got = swap_tensor(mixed_sent, step, levels)
        if step < levels - 1:
            mixed, mixed_sent = add(mixed, got)
        else:
            mixed_rows = add(mixed, got, (bf16,))[0]
        count = 1 if step == levels - 1 else 2
        parts = backward(device, step, slopes, held, bf16, count)
        returned.append([swap_tensor(part, step, levels) for part in parts])
    own = backward(device, None, slopes, held, f32, 1)[0]

    pieces = gather_chips(piece, steps)
    rows_parts = gather_chips(mixed_rows, steps)
    left_total, left_sent = left_partial(early, late, rows_parts, norm_scale)
    left_got = swap_core(left_sent)
    pieces = [pieces, [swap_core(part) for part in pieces]]
    soon = [(side, position) for side in range(2) for position in range(chips - 1)]
    last = [(side, chips - 1) for side in range(2)]
    placed = place(device, chips, [pieces[side][position] for side, position in soon], soon)
    right_grad, left_grad = finish(
        device, chips, placed, left_total, left_got, [pieces[side][-1] for side, _ in last], last
    )
    token_grad = token_total(own, mixed_rows, left_factor, returned)
    return activated, token_grad, left_grad, right_grad


def solution(mesh):
    placed = (
        P("dp", "tensor"),
        P(None, "tensor", None),
        P("tensor", None),
        P(None, "tensor"),
        P("dp", "tensor"),
    )

    return jax.shard_map(
        body,
        mesh=mesh,
        in_specs=placed,
        out_specs=(P("dp", "tensor"), P("dp", "tensor"), P("tensor", None), P(None, "tensor")),
        check_vma=False,
    )
```
